32 devices in a mesh: group: 8 (over y, x, core), member: 4 (over z).
Axes of the slice: x: 2, y: 2, z: 4, core: 2. Of those that a mesh axis runs over, the one named last changes fastest.
Arguments:
- embeddings: bfloat16 [131072, 256], P(('group', 'member')), may hold values from -64 to 64
- cluster_ids: int32 [131072], P(('group', 'member')), may hold values from 0 to 7, as said below
- centroids: bfloat16 [8, 4096, 256], P('group', 'member'), may hold values from -40 to 40
Outputs:
- new_centroids: float32 [8, 4096, 256], P('group', 'member')
- mass: float32 [8, 4096], P('group', 'member')
The draws below stay inside these ranges and needn't reach their ends.
Inputs may be any that keep to these rules, and one draw needn't show every extreme that they name: `cluster_ids`: each device's 4096 rows hold exactly 512 rows of every cluster.
All inputs are finite; a program needn't handle non-finite values.
Results may differ from the reference program's by a relative error of at most 0.0006.
Values may be sent and summed in bfloat16 or wider, within the bound.
No kernel may reach another device: no remote copies, remote signals or barrier semaphores. Data moves between devices by JAX's collectives and lax.ppermute only.
A program may use at most 64 MiB of HBM per device.

```python
import math
import jax
import jax.numpy as jnp
from jax import lax

D = 256
K_SUB = 4096
ROW_DEV = 4096
CLUSTERS = 8
ROWS = 131072


def cluster_table(key):
    device_count = ROWS // ROW_DEV
    keys = jax.random.split(jax.random.fold_in(key, 7), device_count)
    perms = jax.vmap(lambda one_key: jax.random.permutation(one_key, ROW_DEV))(keys)
    return (perms % CLUSTERS).reshape(-1).astype(jnp.int32)


def centre_table(key):
    base = jax.random.normal(jax.random.fold_in(key, 11), (CLUSTERS, K_SUB, D), jnp.float32)
    return jnp.clip(base, -6.0, 6.0)


def draw_cluster_ids(key, part):
    return cluster_table(key)


def draw_centroids(key, part):
    return centre_table(key).astype(jnp.bfloat16)


def draw_embeddings(key, part):
    base = jax.random.normal(jax.random.fold_in(key, 21), (ROWS, D), jnp.float32)
    return jnp.clip(base, -6.0, 6.0).astype(jnp.bfloat16)


def setup_inputs(seed: int = 0) -> dict:
    key_list = jax.random.split(jax.random.key(seed), 4)
    embeddings = draw_embeddings(jax.random.fold_in(key_list[3], 71), 0)
    cluster_ids = draw_cluster_ids(jax.random.fold_in(key_list[3], 71), 0)
    centroids = draw_centroids(jax.random.fold_in(key_list[3], 71), 0)
    return dict(embeddings=embeddings, cluster_ids=cluster_ids, centroids=centroids)


PRIOR_MASS = 1.0

def reference(embeddings, cluster_ids, centroids):
    row_order = jnp.argsort(cluster_ids, stable=True)
    grouped = embeddings[row_order].reshape(CLUSTERS, -1, D)
    norms = lax.optimization_barrier(jnp.sum(jnp.square(centroids.astype(jnp.float32)), axis=-1))
    factor = 2.0 / math.sqrt(D)

    def one_cluster(packed):
        cluster_rows, centres, centre_norms = packed
        row_total = cluster_rows.shape[0]
        block_rows = min(512, row_total)
        blocks = cluster_rows.reshape(row_total // block_rows, block_rows, D)

        def visit(carry, block_x):
            weighted, total_mass = carry
            scores = lax.dot_general(block_x, centres, (((1,), (1,)), ((), ())), preferred_element_type=jnp.float32)
            logits = (scores - 0.5 * centre_norms) * factor
            weights_block = jax.nn.softmax(logits, axis=-1).astype(jnp.bfloat16)
            weighted = weighted + lax.dot_general(weights_block, block_x, (((0,), (0,)), ((), ())), preferred_element_type=jnp.float32)
            total_mass = total_mass + lax.optimization_barrier(jnp.sum(weights_block.astype(jnp.float32), axis=0))
            return ((weighted, total_mass), None)
        start = (jnp.zeros((K_SUB, D), jnp.float32), jnp.zeros((K_SUB,), jnp.float32))
        (weighted, total_mass), _ = lax.scan(visit, start, blocks)
        updated = (weighted + PRIOR_MASS * centres.astype(jnp.float32)) / (total_mass + PRIOR_MASS)[:, None]
        return (updated, total_mass)
    new_centroids, mass = lax.map(one_cluster, (grouped, centroids, norms))
    return (new_centroids, mass)
```

```python
import functools
import math

import jax
import jax.numpy as jnp
from jax import lax
from jax.experimental import pallas as pl
from jax.experimental.pallas import tpu as pltpu
from jax.sharding import PartitionSpec as P

PRIOR_MASS = 1.0
LOG2E = 1.4426950408889634
SEND_SCALE = 512.0
MASS_SCALE = 8.0
PAD = 16
NT = (((1,), (1,)), ((), ()))


def full(shape):
    return pl.BlockSpec(shape, lambda *_: (0,) * len(shape))


def regroup_kernel(ids_ref, x_ref, out_ref, dest_ref):
    lines, width = ids_ref.shape
    clusters = pl.num_programs(0)
    per = out_ref.shape[1]

    @pl.when(pl.program_id(0) == 0)
    def _():
        ids = ids_ref[...]
        upto = (
            lax.broadcasted_iota(jnp.int32, (width, width), 0)
            <= lax.broadcasted_iota(jnp.int32, (width, width), 1)
        )
        upto = jnp.where(upto, 1.0, 0.0).astype(jnp.bfloat16)
        before = (
            lax.broadcasted_iota(jnp.int32, (lines, lines), 1)
            < lax.broadcasted_iota(jnp.int32, (lines, lines), 0)
        )
        before = jnp.where(before, 1.0, 0.0).astype(jnp.bfloat16)
        ones = jnp.ones((width, width), jnp.bfloat16)
        dest = jnp.zeros((lines, width), jnp.float32)
        for c in range(clusters):
            mask = ids == c
            hot = jnp.where(mask, 1.0, 0.0).astype(jnp.bfloat16)
            within = jnp.dot(hot, upto, preferred_element_type=jnp.float32)
            total = jnp.dot(hot, ones, preferred_element_type=jnp.float32)
            ahead = jnp.dot(
                before, total.astype(jnp.bfloat16), preferred_element_type=jnp.float32
            )
            dest = jnp.where(mask, within + ahead + float(c * per - 1), dest)
        dest_ref[...] = dest.astype(jnp.int32)

    first = pl.program_id(0) * per
    slot = lax.broadcasted_iota(jnp.int32, (per, width), 0) + first
    total = jnp.zeros((per, x_ref.shape[1]), jnp.float32)
    for j in range(lines):
        hot = jnp.where(dest_ref[j : j + 1, :] == slot, 1.0, 0.0).astype(jnp.bfloat16)
        total = total + jnp.dot(
            hot, x_ref[j * width : (j + 1) * width, :], preferred_element_type=jnp.float32
        )
    out_ref[0] = total.astype(out_ref.dtype)


def regroup(ids, x, clusters):
    rows, dim = x.shape
    width = 256
    lines = rows // width
    per = rows // clusters
    return pl.pallas_call(
        regroup_kernel,
        grid=(clusters,),
        in_specs=[full((lines, width)), full((rows, dim))],
        out_specs=pl.BlockSpec((1, per, dim), lambda c: (c, 0, 0)),
        out_shape=jax.ShapeDtypeStruct((clusters, per, dim), x.dtype),
        scratch_shapes=[pltpu.VMEM((lines, width), jnp.int32)],
        cost_estimate=pl.CostEstimate(
            flops=2 * rows * rows * dim, bytes_accessed=4 * rows * dim, transcendentals=0
        ),
        name="regroup",
    )(ids.reshape(lines, width), x)


def half_norms(c, factor):
    sq = c.astype(jnp.float32)
    sq = sq * sq
    high = sq.astype(jnp.bfloat16)
    low = (sq - high.astype(jnp.float32)).astype(jnp.bfloat16)
    ones = jnp.ones((8, c.shape[1]), jnp.bfloat16)
    total = lax.dot_general(ones, high, NT, preferred_element_type=jnp.float32)
    total = total + lax.dot_general(ones, low, NT, preferred_element_type=jnp.float32)
    return total[0:1] * (0.5 * factor)


def logits_of(x, c, h, factor):
    s = lax.dot_general(x, c, NT, preferred_element_type=jnp.float32)
    return s * factor - h


def stats_kernel(factor, lanes, members, x_ref, *refs):
    c_refs = refs[:members]
    m_ref, inv_ref, h_ref, l_ref = refs[members:]
    rows = x_ref.shape[0]
    sub = c_refs[0].shape[0]

    @pl.when(pl.program_id(0) == 0)
    def _():
        for j in range(members):
            h_ref[:, j * sub : (j + 1) * sub] = half_norms(c_refs[j][...], factor)

    x = x_ref[...]
    top = None
    for j in range(members):
        for k in range(0, sub, lanes):
            at = j * sub + k
            l = logits_of(x, c_refs[j][k : k + lanes, :], h_ref[:, at : at + lanes], factor)
            l_ref[:, at : at + lanes] = l
            for q in range(0, lanes, 128):
                part = l[:, q : q + 128]
                top = part if top is None else jnp.maximum(top, part)
    top = jnp.max(top, axis=1, keepdims=True)
    top = jnp.broadcast_to(top, (rows, 128))
    total = jnp.zeros((rows, 128), jnp.float32)
    for at in range(0, members * sub, 128):
        total = total + jnp.exp(l_ref[:, at : at + 128] - top)
    total = jnp.broadcast_to(jnp.sum(total, axis=1, keepdims=True), (rows, 128))
    m_ref[...] = top
    inv_ref[...] = 1.0 / total


def stats(x, shards, factor, tile):
    rows, dim = x.shape
    members, sub = len(shards), shards[0].shape[0]
    lanes = min(256, sub)
    wide = pl.BlockSpec((tile, 128), lambda i: (i, 0))
    return pl.pallas_call(
        functools.partial(stats_kernel, factor, lanes, members),
        grid=(rows // tile,),
        in_specs=[pl.BlockSpec((tile, dim), lambda i: (i, 0))] + [full((sub, dim))] * members,
        out_specs=[wide, wide],
        out_shape=[jax.ShapeDtypeStruct((rows, 128), jnp.float32)] * 2,
        scratch_shapes=[
            pltpu.VMEM((1, members * sub), jnp.float32),
            pltpu.VMEM((tile, members * sub), jnp.float32),
        ],
        cost_estimate=pl.CostEstimate(
            flops=2 * rows * members * sub * dim,
            bytes_accessed=2 * dim * (rows + members * sub) + 1024 * rows,
            transcendentals=rows * members * sub,
        ),
        name="stats",
    )(x, *shards)


def weigh_kernel(factor, lanes, send, x_ref, m_ref, inv_ref, c_ref, *refs):
    if send:
        out_ref, h_ref, xt_ref, acc_ref = refs
    else:
        acc_ref, h_ref, xt_ref = refs
    rows, dim = x_ref.shape
    sub = c_ref.shape[0]

    @pl.when(pl.program_id(0) == 0)
    def _():
        h_ref[...] = half_norms(c_ref[...], factor)
        xt_ref[dim:, :] = jnp.ones((PAD, rows), jnp.bfloat16)
        acc_ref[...] = jnp.zeros_like(acc_ref)

    x = x_ref[...]
    xt_ref[:dim, :] = x.T
    xt = xt_ref[...]
    m = jnp.concatenate([m_ref[...]] * (lanes // 128), axis=1)
    inv = jnp.concatenate([inv_ref[...]] * (lanes // 128), axis=1)
    for k in range(0, sub, lanes):
        l = logits_of(x, c_ref[k : k + lanes, :], h_ref[:, k : k + lanes], factor)
        r = (jnp.exp(l - m) * inv).astype(jnp.bfloat16)
        acc_ref[:, k : k + lanes] += jnp.dot(xt, r, preferred_element_type=jnp.float32)

    if send:

        @pl.when(pl.program_id(0) == pl.num_programs(0) - 1)
        def _():
            mass = acc_ref[dim : dim + 1, :]
            scale = SEND_SCALE / jnp.maximum(mass, 1e-30)
            out_ref[:dim, :] = acc_ref[:dim, :] * scale
            mass = mass * MASS_SCALE
            parts = []
            for _ in range(3):
                part = mass.astype(jnp.bfloat16).astype(jnp.float32)
                parts.append(part)
                mass = mass - part
            rest = jnp.zeros((PAD - 3, sub), jnp.float32)
            out_ref[dim:, :] = jnp.concatenate(parts + [rest], axis=0)


def weigh(x, m, inv, c, factor, tile, send):
    rows, dim = x.shape
    sub = c.shape[0]
    lanes = min(256, sub)
    wide = pl.BlockSpec((tile, 128), lambda i: (i, 0))
    acc = (dim + PAD, sub)
    scratch = [pltpu.VMEM((1, sub), jnp.float32), pltpu.VMEM((dim + PAD, tile), jnp.bfloat16)]
    if send:
        scratch.append(pltpu.VMEM(acc, jnp.float32))
    return pl.pallas_call(
        functools.partial(weigh_kernel, factor, lanes, send),
        grid=(rows // tile,),
        in_specs=[pl.BlockSpec((tile, dim), lambda i: (i, 0)), wide, wide, full((sub, dim))],
        out_specs=full(acc),
        out_shape=jax.ShapeDtypeStruct(acc, jnp.float32),
        scratch_shapes=scratch,
        cost_estimate=pl.CostEstimate(
            flops=4 * rows * sub * dim,
            bytes_accessed=2 * dim * (rows + sub) + 1024 * rows,
            transcendentals=rows * sub,
        ),
        name="weigh",
    )(x, m, inv, c)


def finish_kernel(own_ref, c_ref, *refs):
    arrived, out_ref, mass_ref = refs[:-2], refs[-2], refs[-1]
    dim = c_ref.shape[1]
    total = own_ref[:dim, :]
    mass = own_ref[dim : dim + 1, :]
    for ref in arrived:
        parts = ref[dim:, :]
        part = (parts[0:1] + parts[1:2] + parts[2:3]) * (1.0 / MASS_SCALE)
        total = total + ref[:dim, :] * (part * (1.0 / SEND_SCALE))
        mass = mass + part
    mass_ref[...] = mass
    prior = PRIOR_MASS * c_ref[...].astype(jnp.float32)
    inv = 1.0 / (mass + PRIOR_MASS)
    out_ref[...] = (total * inv).T + prior * jnp.broadcast_to(inv, (8, inv.shape[1])).T[:, 0:1]


def finish(own, c, arrived):
    sub, dim = c.shape
    return pl.pallas_call(
        finish_kernel,
        out_shape=[
            jax.ShapeDtypeStruct((sub, dim), jnp.float32),
            jax.ShapeDtypeStruct((1, sub), jnp.float32),
        ],
        name="finish",
    )(own, c, *arrived)


def local(embeddings, cluster_ids, centroids):
    rows, dim = embeddings.shape
    clusters = lax.axis_size("group")
    members = lax.axis_size("member")
    factor = 2.0 / math.sqrt(dim)
    own = centroids[0]

    def rotate(value, step):
        return lax.ppermute(
            value, "member", [(i, (i + step) % members) for i in range(members)]
        )

    order = sorted(range(1, members), key=lambda d: abs(d - members / 2))
    arrived = {d: rotate(own, d) for d in order}
    packed = regroup(cluster_ids, embeddings, clusters)
    x = lax.all_to_all(packed, "group", split_axis=0, concat_axis=0, tiled=True)
    x = x.reshape(rows, dim)
    m, inv = stats(x, [own] + [arrived[d] for d in order], factor, min(256, rows))
    tile = min(512, rows)
    back = []
    for d in order:
        partial = weigh(x, m, inv, arrived[d], factor, tile, True).astype(jnp.float16)
        back.append(rotate(partial, -d).astype(jnp.float32))
    mine = weigh(x, m, inv, own, factor, tile, False)
    updated, mass = finish(mine, own, back)
    return updated[None], mass


def solution(mesh):
    placed = (P(("group", "member"), None), P(("group", "member")), P("group", "member", None))
    return jax.shard_map(
        local,
        mesh=mesh,
        in_specs=placed,
        out_specs=(P("group", "member", None), P("group", "member")),
        check_vma=False,
    )
```

```python
import functools
import math

import jax
import jax.numpy as jnp
from jax import lax
from jax.experimental import pallas as pl
from jax.experimental.pallas import tpu as pltpu
from jax.sharding import PartitionSpec as P


PRIOR_MASS = 1.0
SEND_SCALE = 512.0
MASS_SCALE = 8.0
PAD = 16
NT = (((1,), (1,)), ((), ()))


def regroup_kernel(ids_ref, x_ref, out_ref, dest_ref):
    lines, width = ids_ref.shape
    clusters, per, dim = out_ref.shape
    ids = ids_ref[...]
    upto = (
        lax.broadcasted_iota(jnp.int32, (width, width), 0)
        <= lax.broadcasted_iota(jnp.int32, (width, width), 1)
    )
    upto = jnp.where(upto, 1.0, 0.0).astype(jnp.bfloat16)
    before = (
        lax.broadcasted_iota(jnp.int32, (lines, lines), 1)
        < lax.broadcasted_iota(jnp.int32, (lines, lines), 0)
    )
    before = jnp.where(before, 1.0, 0.0).astype(jnp.bfloat16)
    ones = jnp.ones((width, width), jnp.bfloat16)
    dest = jnp.zeros((lines, width), jnp.float32)
    for c in range(clusters):
        mask = ids == c
        hot = jnp.where(mask, 1.0, 0.0).astype(jnp.bfloat16)
        within = jnp.dot(hot, upto, preferred_element_type=jnp.float32)
        total = jnp.dot(hot, ones, preferred_element_type=jnp.float32)
        ahead = jnp.dot(before, total.astype(jnp.bfloat16), preferred_element_type=jnp.float32)
        dest = jnp.where(mask, within + ahead + float(c * per - 1), dest)
    dest_ref[...] = dest.astype(jnp.int32)

    @pl.loop(0, clusters)
    def _(c):
        slot = lax.broadcasted_iota(jnp.int32, (per, 2 * width), 0) + c * per
        total = jnp.zeros((per, dim), jnp.float32)
        for j in range(0, lines, 2):
            row = jnp.concatenate([dest_ref[j : j + 1, :], dest_ref[j + 1 : j + 2, :]], axis=1)
            hot = jnp.where(row == slot, 1.0, 0.0).astype(jnp.bfloat16)
            total = total + jnp.dot(
                hot, x_ref[j * width : (j + 2) * width, :], preferred_element_type=jnp.float32
            )
        out_ref[c] = total.astype(out_ref.dtype)


def regroup(ids, x, clusters):
    rows, dim = x.shape
    width = 128
    lines = rows // width
    return pl.pallas_call(
        regroup_kernel,
        out_shape=jax.ShapeDtypeStruct((clusters, rows // clusters, dim), x.dtype),
        scratch_shapes=[pltpu.VMEM((lines, width), jnp.int32)],
        cost_estimate=pl.CostEstimate(
            flops=2 * rows * rows * dim, bytes_accessed=4 * rows * dim, transcendentals=0
        ),
        name="regroup",
    )(ids.reshape(lines, width), x)


def half_norms(c, factor):
    sq = c.astype(jnp.float32)
    sq = sq * sq
    high = sq.astype(jnp.bfloat16)
    low = (sq - high.astype(jnp.float32)).astype(jnp.bfloat16)
    ones = jnp.ones((8, c.shape[1]), jnp.bfloat16)
    total = lax.dot_general(ones, high, NT, preferred_element_type=jnp.float32)
    total = total + lax.dot_general(ones, low, NT, preferred_element_type=jnp.float32)
    return total[0:1] * (0.5 * factor)


def logits_of(x, c, h, factor):
    s = lax.dot_general(x, c, NT, preferred_element_type=jnp.float32)
    return s * factor - h


def stats_kernel(factor, lanes, tile, members, merge, last, x_ref, *refs):
    c_refs = refs[:members]
    old_ref = refs[members] if merge else None
    st_ref, h_ref, l_ref = refs[-3:]
    sub = c_refs[0].shape[0]
    for j in range(members):
        h_ref[:, j * sub : (j + 1) * sub] = half_norms(c_refs[j][...], factor)
    lane = lax.broadcasted_iota(jnp.int32, (tile, 128), 1)

    @pl.loop(0, x_ref.shape[0] // tile)
    def _(i):
        at_rows = pl.ds(pl.multiple_of(i * tile, tile), tile)
        x = x_ref[at_rows, :]
        top = None
        for j in range(members):
            for k in range(0, sub, lanes):
                at = j * sub + k
                l = logits_of(x, c_refs[j][k : k + lanes, :], h_ref[:, at : at + lanes], factor)
                l_ref[:, at : at + lanes] = l
                for q in range(0, lanes, 128):
                    part = l[:, q : q + 128]
                    top = part if top is None else jnp.maximum(top, part)
        top = jnp.broadcast_to(jnp.max(top, axis=1, keepdims=True), (tile, 128))
        if merge:
            old = old_ref[at_rows, :]
            old_top = jnp.broadcast_to(old[:, 0:1], (tile, 128))
            old_sum = jnp.broadcast_to(old[:, 1:2], (tile, 128))
            top = jnp.maximum(top, old_top)
        total = jnp.zeros((tile, 128), jnp.float32)
        for at in range(0, members * sub, 128):
            total = total + jnp.exp(l_ref[:, at : at + 128] - top)
        total = jnp.broadcast_to(jnp.sum(total, axis=1, keepdims=True), (tile, 128))
        if merge:
            total = total + old_sum * jnp.exp(old_top - top)
        if last:
            total = 1.0 / total
        st_ref[at_rows, :] = jnp.where(lane == 0, top, total)


def stats(x, shards, factor, tile, old, last):
    rows, dim = x.shape
    members, sub = len(shards), shards[0].shape[0]
    lanes = min(256, sub)
    merge = old is not None
    return pl.pallas_call(
        functools.partial(stats_kernel, factor, lanes, tile, members, merge, last),
        out_shape=jax.ShapeDtypeStruct((rows, 128), jnp.float32),
        scratch_shapes=[
            pltpu.VMEM((1, members * sub), jnp.float32),
            pltpu.VMEM((tile, members * sub), jnp.float32),
        ],
        cost_estimate=pl.CostEstimate(
            flops=2 * rows * members * sub * dim,
            bytes_accessed=2 * dim * (rows + members * sub) + 1024 * rows,
            transcendentals=rows * members * sub,
        ),
        name="stats",
    )(x, *shards, *([old] if merge else []))


def weigh_kernel(factor, lanes, tile, send, x_ref, st_ref, c_ref, *refs):
    if send:
        out_ref, h_ref, xt_ref, acc_ref = refs
    else:
        acc_ref, h_ref, xt_ref = refs
    dim = x_ref.shape[1]
    sub = c_ref.shape[0]
    h_ref[...] = half_norms(c_ref[...], factor)
    xt_ref[dim:, :] = jnp.ones((PAD, tile), jnp.bfloat16)
    acc_ref[...] = jnp.zeros_like(acc_ref)

    @pl.loop(0, x_ref.shape[0] // tile)
    def _(i):
        at_rows = pl.ds(pl.multiple_of(i * tile, tile), tile)
        x = x_ref[at_rows, :]
        xt_ref[:dim, :] = x.T
        xt = xt_ref[...]
        m = jnp.broadcast_to(st_ref[at_rows, 0:1], (tile, lanes))
        inv = jnp.broadcast_to(st_ref[at_rows, 1:2], (tile, lanes))
        for k in range(0, sub, lanes):
            l = logits_of(x, c_ref[k : k + lanes, :], h_ref[:, k : k + lanes], factor)
            r = (jnp.exp(l - m) * inv).astype(jnp.bfloat16)
            acc_ref[:, k : k + lanes] += jnp.dot(xt, r, preferred_element_type=jnp.float32)

    if send:
        mass = acc_ref[dim : dim + 1, :]
        scale = SEND_SCALE / jnp.maximum(mass, 1e-30)
        out_ref[:dim, :] = acc_ref[:dim, :] * scale
        mass = mass * MASS_SCALE
        parts = []
        for _ in range(3):
            part = mass.astype(jnp.bfloat16).astype(jnp.float32)
            parts.append(part)
            mass = mass - part
        rest = jnp.zeros((PAD - 3, sub), jnp.float32)
        out_ref[dim:, :] = jnp.concatenate(parts + [rest], axis=0)


def weigh(x, st, c, factor, tile, send):
    rows, dim = x.shape
    sub = c.shape[0]
    lanes = min(256, sub)
    acc = (dim + PAD, sub)
    scratch = [pltpu.VMEM((1, sub), jnp.float32), pltpu.VMEM((dim + PAD, tile), jnp.bfloat16)]
    if send:
        scratch.append(pltpu.VMEM(acc, jnp.float32))
    return pl.pallas_call(
        functools.partial(weigh_kernel, factor, lanes, tile, send),
        out_shape=jax.ShapeDtypeStruct(acc, jnp.float32),
        scratch_shapes=scratch,
        cost_estimate=pl.CostEstimate(
            flops=4 * rows * sub * dim,
            bytes_accessed=2 * dim * (rows + sub) + 1024 * rows,
            transcendentals=rows * sub,
        ),
        name="weigh",
    )(x, st, c)


def finish_kernel(own_ref, c_ref, *refs):
    arrived, out_ref, mass_ref = refs[:-2], refs[-2], refs[-1]
    dim = c_ref.shape[1]
    total = own_ref[:dim, :]
    mass = own_ref[dim : dim + 1, :]
    for ref in arrived:
        parts = ref[dim:, :]
        part = (parts[0:1] + parts[1:2] + parts[2:3]) * (1.0 / MASS_SCALE)
        total = total + ref[:dim, :] * (part * (1.0 / SEND_SCALE))
        mass = mass + part
    mass_ref[...] = mass
    prior = PRIOR_MASS * c_ref[...].astype(jnp.float32)
    inv = 1.0 / (mass + PRIOR_MASS)
    out_ref[...] = (total * inv).T + prior * jnp.broadcast_to(inv, (8, inv.shape[1])).T[:, 0:1]


def finish(own, c, arrived):
    sub, dim = c.shape
    return pl.pallas_call(
        finish_kernel,
        out_shape=[
            jax.ShapeDtypeStruct((sub, dim), jnp.float32),
            jax.ShapeDtypeStruct((1, sub), jnp.float32),
        ],
        name="finish",
    )(own, c, *arrived)


def local(embeddings, cluster_ids, centroids):
    rows, dim = embeddings.shape
    clusters = lax.axis_size("group")
    members = lax.axis_size("member")
    factor = 2.0 / math.sqrt(dim)
    own = centroids[0]

    def rotate(value, step):
        return lax.ppermute(
            value, "member", [(i, (i + step) % members) for i in range(members)]
        )

    tile = min(512, rows)
    order = sorted(range(1, members), key=lambda d: abs(d - members / 2))
    arrived = {}
    for d in order:
        arrived[d] = rotate(own, d)
    packed = regroup(cluster_ids, embeddings, clusters)
    x = lax.all_to_all(packed, "group", split_axis=0, concat_axis=0, tiled=True)
    x = x.reshape(rows, dim)
    st = stats(x, [own] + [arrived[d] for d in order[:-1]], factor, tile, None, members == 1)
    for d in order[-1:]:
        st = stats(x, [arrived[d]], factor, tile, st, True)
    back = []
    for d in order:
        partial = weigh(x, st, arrived[d], factor, tile, True).astype(jnp.float16)
        back.append(rotate(partial, -d).astype(jnp.float32))
    mine = weigh(x, st, own, factor, tile, False)
    updated, mass = finish(mine, own, back)
    return updated[None], mass


def solution(mesh):
    placed = (P(("group", "member"), None), P(("group", "member")), P("group", "member", None))
    return jax.shard_map(
        local,
        mesh=mesh,
        in_specs=placed,
        out_specs=(P("group", "member", None), P("group", "member")),
        check_vma=False,
    )
```

```python
import functools
import math

import jax
import jax.numpy as jnp
from jax import lax
from jax.experimental import pallas as pl
from jax.experimental.pallas import tpu as pltpu
from jax.sharding import PartitionSpec as P


PRIOR_MASS = 1.0
SEND_SCALE = 512.0
MASS_SCALE = 8.0
PAD = 16
VMEM = 24 << 20
NT = (((1,), (1,)), ((), ()))


def regroup_kernel(ids_ref, x_ref, out_ref, dest_ref):
    lines, width = ids_ref.shape
    clusters, per, dim = out_ref.shape
    ids = ids_ref[...]
    upto = (
        lax.broadcasted_iota(jnp.int32, (width, width), 0)
        <= lax.broadcasted_iota(jnp.int32, (width, width), 1)
    )
    upto = jnp.where(upto, 1.0, 0.0).astype(jnp.bfloat16)
    before = (
        lax.broadcasted_iota(jnp.int32, (lines, lines), 1)
        < lax.broadcasted_iota(jnp.int32, (lines, lines), 0)
    )
    before = jnp.where(before, 1.0, 0.0).astype(jnp.bfloat16)
    ones = jnp.ones((width, width), jnp.bfloat16)
    dest = jnp.zeros((lines, width), jnp.float32)
    for c in range(clusters):
        mask = ids == c
        hot = jnp.where(mask, 1.0, 0.0).astype(jnp.bfloat16)
        within = jnp.dot(hot, upto, preferred_element_type=jnp.float32)
        total = jnp.dot(hot, ones, preferred_element_type=jnp.float32)
        ahead = jnp.dot(before, total.astype(jnp.bfloat16), preferred_element_type=jnp.float32)
        dest = jnp.where(mask, within + ahead + float(c * per - 1), dest)
    dest_ref[...] = dest.astype(jnp.int32)

    @pl.loop(0, clusters)
    def _(c):
        slot = lax.broadcasted_iota(jnp.int32, (per, 2 * width), 0) + c * per
        total = jnp.zeros((per, dim), jnp.float32)
        for j in range(0, lines, 2):
            row = jnp.concatenate([dest_ref[j : j + 1, :], dest_ref[j + 1 : j + 2, :]], axis=1)
            hot = jnp.where(row == slot, 1.0, 0.0).astype(jnp.bfloat16)
            total = total + jnp.dot(
                hot, x_ref[j * width : (j + 2) * width, :], preferred_element_type=jnp.float32
            )
        out_ref[c] = total.astype(out_ref.dtype)


def regroup(ids, x, clusters):
    rows, dim = x.shape
    width = 128
    lines = rows // width
    return pl.pallas_call(
        regroup_kernel,
        out_shape=jax.ShapeDtypeStruct((clusters, rows // clusters, dim), x.dtype),
        scratch_shapes=[pltpu.VMEM((lines, width), jnp.int32)],
        compiler_params=pltpu.CompilerParams(vmem_limit_bytes=VMEM),
        cost_estimate=pl.CostEstimate(
            flops=2 * rows * rows * dim, bytes_accessed=4 * rows * dim, transcendentals=0
        ),
        name="regroup",
    )(ids.reshape(lines, width), x)


def squares(v):
    sq = v.astype(jnp.float32)
    sq = sq * sq
    high = sq.astype(jnp.bfloat16)
    return high, (sq - high.astype(jnp.float32)).astype(jnp.bfloat16)


def half_norms(c, factor):
    ones = jnp.ones((c.shape[1], 128), jnp.bfloat16)
    high, low = squares(c)
    total = jnp.dot(high, ones, preferred_element_type=jnp.float32)
    total = total + jnp.dot(low, ones, preferred_element_type=jnp.float32)
    return total * (0.5 * factor)


def row_bounds(x, factor):
    ones = jnp.ones((8, x.shape[1]), jnp.bfloat16)
    high, low = squares(x)
    total = lax.dot_general(ones, high, NT, preferred_element_type=jnp.float32)
    total = total + lax.dot_general(ones, low, NT, preferred_element_type=jnp.float32)
    return total[0:1] * (0.5 * factor)


def logits_of(c, x, h, factor):
    s = lax.dot_general(c, x, NT, preferred_element_type=jnp.float32)
    return s * factor - jnp.concatenate([h] * (x.shape[0] // 128), axis=1)


def fold(value, op):
    rows, cols = value.shape
    return op(value.reshape(rows // 8, 8, cols), axis=0)


def stats_kernel(factor, step, tile, members, merge, rest, x_ref, *refs):
    c_refs, refs = refs[:members], refs[members:]
    old_ref, refs = (refs[0], refs[1:]) if merge else (None, refs)
    rest_refs, refs = refs[:rest], refs[rest:]
    st_ref, h_ref = refs[:2]
    sub = c_refs[0].shape[0]
    rows = x_ref.shape[0]
    last = len(refs) > 2
    for j in range(members):
        h_ref[j * sub : (j + 1) * sub, :] = half_norms(c_refs[j][...], factor)

    @pl.loop(0, rows // tile)
    def _(i):
        at = pl.ds(pl.multiple_of(i * tile, tile), tile)
        x = x_ref[at, :]
        if merge:
            bound = old_ref[0:1, at]
            total = old_ref[1:2, at]
        else:
            bound = row_bounds(x, factor)
            total = jnp.zeros((1, tile), jnp.float32)
        wide = jnp.zeros((8, tile), jnp.float32)
        for j in range(members):
            for k in range(0, sub, step):
                h = h_ref[j * sub + k : j * sub + k + step, :]
                l = logits_of(c_refs[j][k : k + step, :], x, h, factor)
                wide = wide + fold(jnp.exp(l - bound), jnp.sum)
        st_ref[0:1, at] = bound
        st_ref[1:2, at] = total + jnp.sum(wide, axis=0, keepdims=True)

    if not last:
        return
    buf_ref, l_ref = refs[2:]

    @pl.when(jnp.min(st_ref[1:2, :]) < 1e-24)
    def _():
        st_ref[0:1, :] = jnp.full((1, rows), -3e38, jnp.float32)
        st_ref[1:2, :] = jnp.zeros((1, rows), jnp.float32)
        for ref in tuple(c_refs) + tuple(rest_refs):
            pltpu.sync_copy(ref, buf_ref)
            h_ref[0:sub, :] = half_norms(buf_ref[...], factor)

            @pl.loop(0, rows // 128)
            def _(i):
                at = pl.ds(pl.multiple_of(i * 128, 128), 128)
                l_ref[...] = logits_of(buf_ref[...], x_ref[at, :], h_ref[0:sub, :], factor)
                was = st_ref[0:1, at]
                top = jnp.max(fold(l_ref[...], jnp.max), axis=0, keepdims=True)
                top = jnp.maximum(top, was)
                total = fold(jnp.exp(l_ref[...] - top), jnp.sum)
                total = jnp.sum(total, axis=0, keepdims=True)
                st_ref[0:1, at] = top
                st_ref[1:2, at] = total + st_ref[1:2, at] * jnp.exp(was - top)

    st_ref[1:2, :] = 1.0 / st_ref[1:2, :]


def stats(x, shards, factor, tile, old=None, rest=None):
    rows, dim = x.shape
    members, sub = len(shards), shards[0].shape[0]
    step = min(256, sub)
    merge, last = old is not None, rest is not None
    rest = rest or []
    whole = pl.BlockSpec(memory_space=pltpu.VMEM)
    scratch = [pltpu.VMEM((members * sub, 128), jnp.float32)]
    if last:
        scratch += [pltpu.VMEM((sub, dim), jnp.bfloat16), pltpu.VMEM((sub, 128), jnp.float32)]
    return pl.pallas_call(
        functools.partial(stats_kernel, factor, step, tile, members, merge, len(rest)),
        in_specs=[whole] * (1 + members + merge) + [pl.BlockSpec(memory_space=pl.ANY)] * len(rest),
        out_specs=whole,
        out_shape=jax.ShapeDtypeStruct((8, rows), jnp.float32),
        scratch_shapes=scratch,
        compiler_params=pltpu.CompilerParams(vmem_limit_bytes=VMEM),
        cost_estimate=pl.CostEstimate(
            flops=2 * rows * members * sub * dim,
            bytes_accessed=2 * dim * (rows + members * sub),
            transcendentals=rows * members * sub,
        ),
        name="stats",
    )(x, *shards, *([old] if merge else []), *rest)


def weigh_kernel(factor, step, tile, send, x_ref, st_ref, c_ref, *refs):
    if send:
        out_ref, h_ref, acc_ref, mass_ref = refs
    else:
        acc_ref, mass_ref, h_ref = refs
    dim = x_ref.shape[1]
    sub = c_ref.shape[0]
    h_ref[...] = half_norms(c_ref[...], factor)
    acc_ref[...] = jnp.zeros_like(acc_ref)
    mass_ref[...] = jnp.zeros_like(mass_ref)

    @pl.loop(0, x_ref.shape[0] // tile)
    def _(i):
        at = pl.ds(pl.multiple_of(i * tile, tile), tile)
        x = x_ref[at, :]
        top = st_ref[0:1, at]
        inv = st_ref[1:2, at]
        for k in range(0, sub, step):
            ks = slice(k, k + step)
            l = logits_of(c_ref[ks, :], x, h_ref[ks, :], factor)
            r = (jnp.exp(l - top) * inv).astype(jnp.bfloat16)
            acc_ref[ks, :] += jnp.dot(r, x, preferred_element_type=jnp.float32)
            r = r.astype(jnp.float32)
            part = r[:, 0:128]
            for q in range(128, tile, 128):
                part = part + r[:, q : q + 128]
            mass_ref[ks, :] += part

    mass = jnp.broadcast_to(jnp.sum(mass_ref[...], axis=1, keepdims=True), (sub, 128))
    if not send:
        mass_ref[...] = mass
        return
    scale = jnp.concatenate([SEND_SCALE / jnp.maximum(mass, 1e-30)] * (dim // 128), axis=1)
    out_ref[0:sub, :] = acc_ref[...] * scale
    mass = mass.T[0:1, :] * MASS_SCALE
    parts = []
    for _ in range(3):
        part = mass.astype(jnp.bfloat16).astype(jnp.float32)
        parts += [part[:, k : k + dim] for k in range(0, sub, dim)]
        mass = mass - part
    rest = out_ref.shape[0] - sub - len(parts)
    parts.append(jnp.zeros((rest, dim), jnp.float32))
    out_ref[sub:, :] = jnp.concatenate(parts, axis=0)


def weigh(x, st, c, factor, tile, send):
    rows, dim = x.shape
    sub = c.shape[0]
    step = min(256, sub)
    sums, masses = (sub, dim), (sub, 128)
    scratch = [pltpu.VMEM((sub, 128), jnp.float32)]
    if send:
        scratch += [pltpu.VMEM(sums, jnp.float32), pltpu.VMEM(masses, jnp.float32)]
        out = jax.ShapeDtypeStruct((sub + PAD, dim), jnp.float32)
    else:
        out = [jax.ShapeDtypeStruct(sums, jnp.float32), jax.ShapeDtypeStruct(masses, jnp.float32)]
    return pl.pallas_call(
        functools.partial(weigh_kernel, factor, step, tile, send),
        out_shape=out,
        scratch_shapes=scratch,
        compiler_params=pltpu.CompilerParams(vmem_limit_bytes=VMEM),
        cost_estimate=pl.CostEstimate(
            flops=4 * rows * sub * dim,
            bytes_accessed=2 * dim * (rows + sub),
            transcendentals=rows * sub,
        ),
        name="weigh",
    )(x, st, c)


def finish_kernel(own_ref, own_mass_ref, c_ref, *refs):
    arrived, out_ref, mass_ref = refs[:-2], refs[-2], refs[-1]
    sub, dim = c_ref.shape

    def wide(value):
        return jnp.concatenate([value] * (dim // 128), axis=1)

    total = own_ref[...]
    mass = own_mass_ref[...]
    for ref in arrived:
        count = sub // dim
        part = None
        for p in range(3):
            row = [ref[sub + p * count + q : sub + p * count + q + 1, :] for q in range(count)]
            row = jnp.concatenate(row, axis=1)
            part = row if part is None else part + row
        part = jnp.broadcast_to(part * (1.0 / MASS_SCALE), (128, sub)).T
        total = total + ref[0:sub, :] * wide(part * (1.0 / SEND_SCALE))
        mass = mass + part
    mass_ref[...] = mass.T[0:1, :]
    prior = PRIOR_MASS * c_ref[...].astype(jnp.float32)
    out_ref[...] = (total + prior) * wide(1.0 / (mass + PRIOR_MASS))


def finish(own, own_mass, c, arrived):
    sub, dim = c.shape
    return pl.pallas_call(
        finish_kernel,
        out_shape=[
            jax.ShapeDtypeStruct((sub, dim), jnp.float32),
            jax.ShapeDtypeStruct((1, sub), jnp.float32),
        ],
        compiler_params=pltpu.CompilerParams(vmem_limit_bytes=VMEM),
        name="finish",
    )(own, own_mass, c, *arrived)


def send_order(members):
    return sorted(range(1, members), key=lambda d: abs(d - members / 2))


def local(embeddings, cluster_ids, centroids):
    rows, dim = embeddings.shape
    clusters = lax.axis_size("group")
    members = lax.axis_size("member")
    factor = 2.0 / math.sqrt(dim)
    own = centroids[0]

    def rotate(value, step):
        return lax.ppermute(
            value, "member", [(i, (i + step) % members) for i in range(members)]
        )

    tile = min(1024, rows)
    order = send_order(members)
    arrived = {}
    for d in order:
        arrived[d] = rotate(own, d)
    packed = regroup(cluster_ids, embeddings, clusters)
    x = lax.all_to_all(packed, "group", split_axis=0, concat_axis=0, tiled=True)
    x = x.reshape(rows, dim)
    if members == 1:
        st = stats(x, [own], factor, tile, None, [])
    else:
        early = [own] + [arrived[d] for d in order[:-1]]
        st = stats(x, early, factor, tile)
        st = stats(x, [arrived[order[-1]]], factor, tile, st, early)
    back = []
    for d in order:
        partial = weigh(x, st, arrived[d], factor, tile, True).astype(jnp.float16)
        back.append(rotate(partial, -d).astype(jnp.float32))
    mine, mine_mass = weigh(x, st, own, factor, tile, False)
    updated, mass = finish(mine, mine_mass, own, back)
    return updated[None], mass


def solution(mesh):
    placed = (P(("group", "member"), None), P(("group", "member")), P("group", "member", None))
    return jax.shard_map(
        local,
        mesh=mesh,
        in_specs=placed,
        out_specs=(P("group", "member", None), P("group", "member")),
        check_vma=False,
    )
```
